32 devices in a mesh: atm: 8 (over z, y), ocn: 4 (over x, core).
Axes of the slice: x: 2, y: 2, z: 4, core: 2. Of those that a mesh axis runs over, the one named last changes fastest.
Arguments:
- atm_fields: bfloat16 [4096, 24, 128], P(('atm', 'ocn')), may hold values from -6 to 6
- fwd_blocks: bfloat16 [6144, 128, 128], P(('atm', 'ocn')), may hold values from -0.21875 to 0.21875
- fwd_src_tile: int32 [6144], P(('atm', 'ocn')), may hold values from 0 to 127
- fwd_dst_dev: int32 [6144, 1], P(('atm', 'ocn')), may hold values from 0 to 31, as said below
- fwd_dst_tile: int32 [6144], P(('atm', 'ocn')), may hold values from 0 to 7
- ocean_state: float32 [256, 24, 128], P(('atm', 'ocn')), may hold values from -6 to 6
- wet_mask: int32 [256, 128], P(('atm', 'ocn')), may hold values 0 or 1
- back_blocks: bfloat16 [6144, 128, 128], P(('atm', 'ocn')), may hold values from -0.3125 to 0.3125
- back_src_dev: int32 [6144, 1], P(('atm', 'ocn')), may hold values from 0 to 31, as said below
- back_src_tile: int32 [6144], P(('atm', 'ocn')), may hold values from 0 to 7
- back_dst_tile: int32 [6144], P(('atm', 'ocn')), may hold values from 0 to 127
Outputs:
- ocean_import: float32 [256, 24, 128], P(('atm', 'ocn'))
- atm_import: float32 [4096, 24, 128], P(('atm', 'ocn'))
The draws below stay inside these ranges and needn't reach their ends.
Inputs may be any that keep to these rules, and one draw needn't show every extreme that they name: `fwd_dst_dev`: device d has atm index d // 4 and ocn index d % 4; the device named by a block of device b // 192 differs from it by at most one in each index, counted with wrap-around (nine neighbours, itself included). Among the 192 blocks of one device at most 48 name the same device, and on every device exactly one device is named 48 times. `back_src_dev`: device d has atm index d // 4 and ocn index d % 4; the device named by a block of device b // 192 differs from it by at most one in each index, counted with wrap-around (nine neighbours, itself included). Among the 192 blocks of one device at most 48 name the same device, and on every device exactly one device is named 48 times.
All inputs are finite; a program needn't handle non-finite values. No bound on the sum of `wet_mask` on one device may be relied on, other than what follows from the above.
Results may differ from the reference program's by a relative error of at most 0.0022.
Values may be sent and summed in bfloat16 or wider, within the bound.
No kernel may reach another device: no remote copies, remote signals or barrier semaphores. Data moves between devices by JAX's collectives and lax.ppermute only.
A program may use at most 128 MiB of HBM per device.

```python
import jax
import jax.numpy as jnp
import numpy as np
from jax import lax

C = 128
F = 24
ATM_DEV = 128
OCN_DEV = 8
BLK_DEV = 192
BLOCKS = 6144
ATM_TILES = 4096
OCEAN_TILES = 256
N_OCN = 4
DEVICES = 32


def near_owners(key):
    unit = BLK_DEV // 24
    pattern = jnp.asarray(np.repeat(np.repeat(np.arange(9), [6, 5, 4, 3, 2, 1, 1, 1, 1]), unit), dtype=jnp.int32)
    n_atmos = DEVICES // N_OCN

    def one_device(device_key, device):
        first_key, second_key = jax.random.split(device_key)
        shuffle = jax.random.permutation(first_key, 9).astype(jnp.int32)
        chosen = jax.random.permutation(second_key, shuffle[pattern]).astype(jnp.int32)
        row_step = chosen // 3 - 1
        col_step = chosen % 3 - 1
        here_row = device // N_OCN
        here_col = device % N_OCN
        owner = (here_row + row_step) % n_atmos * N_OCN + (here_col + col_step) % N_OCN
        return owner.astype(jnp.int32)
    device_keys = jax.random.split(key, DEVICES)
    owners = jax.vmap(one_device)(device_keys, jnp.arange(DEVICES, dtype=jnp.int32))
    return owners.reshape(BLOCKS, 1).astype(jnp.int32)


def draw_fwd_dst_dev(key, part):
    return near_owners(jax.random.fold_in(key, 11))


def draw_back_src_dev(key, part):
    return near_owners(jax.random.fold_in(key, 23))


def with_ends(entries, rng, low, top_value):
    extent = entries.shape
    place = [jax.random.randint(jax.random.fold_in(rng, axis), (), 0, extent[axis]) for axis in range(len(extent))]
    entries = entries.at[tuple(place)].set(low)
    longest = extent.index(max(extent))
    place[longest] = (place[longest] + 1) % extent[longest]
    return entries.at[tuple(place)].set(top_value)


def levels(own_key, extent, shards, least, high):
    gain, own = 1.0, jax.random.fold_in(own_key, 6)
    for axis_at, blocks in shards:
        steps = jnp.exp(jax.random.uniform(jax.random.fold_in(own, axis_at), (blocks,), jnp.float32, least / len(shards), high / len(shards)))
        gain = gain * jnp.repeat(steps, extent[axis_at] // blocks).reshape([-1 if axis == axis_at else 1 for axis in range(len(extent))])
    return gain


def gaussian(key, extent, width, bound, cuts=(), kind=jnp.bfloat16):
    entries = jax.random.normal(key, extent, jnp.float32) * width
    if len(cuts) > 0:
        entries = levels(key, extent, cuts, -0.22, 0.18) * entries
    return jnp.clip(entries, min=-bound, max=bound).astype(kind)


def setup_inputs(seed: int = 0) -> dict:
    seeds = jax.random.split(jax.random.key(seed), 12)
    return {
        "atm_fields": gaussian(seeds[0], (ATM_TILES, F, C), 1.0, 6.0, ((0, 32),)),
        "fwd_blocks": gaussian(seeds[1], (BLOCKS, C, C), (6 * C) ** -0.5, 0.21875, ((0, 32),)),
        "fwd_src_tile": with_ends(jax.random.randint(seeds[2], (BLOCKS,), 0, ATM_DEV), jax.random.fold_in(seeds[2], 1), 0, ATM_DEV - 1).astype(jnp.int32),
        "fwd_dst_dev": draw_fwd_dst_dev(jax.random.fold_in(seeds[11], 71), 0),
        "fwd_dst_tile": with_ends(jax.random.randint(seeds[4], (BLOCKS,), 0, OCN_DEV), jax.random.fold_in(seeds[4], 1), 0, OCN_DEV - 1).astype(jnp.int32),
        "ocean_state": gaussian(seeds[5], (OCEAN_TILES, F, C), 1.0, 6.0, ((0, 32),), jnp.float32),
        "wet_mask": with_ends((jax.random.randint(seeds[6], (OCEAN_TILES, C), 0, 4) < 3).astype(jnp.int32), jax.random.fold_in(seeds[6], 1), 0, 1),
        "back_blocks": gaussian(seeds[7], (BLOCKS, C, C), (3 * C) ** -0.5, 0.3125, ((0, 32),)),
        "back_src_dev": draw_back_src_dev(jax.random.fold_in(seeds[11], 71), 0),
        "back_src_tile": with_ends(jax.random.randint(seeds[9], (BLOCKS,), 0, OCN_DEV), jax.random.fold_in(seeds[9], 1), 0, OCN_DEV - 1).astype(jnp.int32),
        "back_dst_tile": with_ends(jax.random.randint(seeds[10], (BLOCKS,), 0, ATM_DEV), jax.random.fold_in(seeds[10], 1), 0, ATM_DEV - 1).astype(jnp.int32),
    }


def block_products(sources, weights):
    def one(pair):
        left, right = pair
        return jnp.einsum("bfi,bij->bfj", left.astype(jnp.float32), right.astype(jnp.float32))
    return lax.map(one, (sources.reshape(DEVICES, BLK_DEV, F, C), weights.reshape(DEVICES, BLK_DEV, C, C))).reshape(BLOCKS, F, C)


def reference(atm_fields, fwd_blocks, fwd_src_tile, fwd_dst_dev, fwd_dst_tile, ocean_state, wet_mask, back_blocks, back_src_dev, back_src_tile, back_dst_tile):
    owner_dev = (jnp.arange(BLOCKS, dtype=jnp.int32) // BLK_DEV).astype(jnp.int32)
    source_rows = (owner_dev * ATM_DEV + fwd_src_tile).astype(jnp.int32)
    fwd_part = block_products(atm_fields[source_rows], fwd_blocks)
    target_rows = (fwd_dst_dev[:, 0] * OCN_DEV + fwd_dst_tile).astype(jnp.int32)
    ocean_import = jax.ops.segment_sum(fwd_part, target_rows, num_segments=OCEAN_TILES)
    wet = wet_mask.astype(jnp.float32)[:, None, :]
    response = (wet * jnp.tanh(ocean_state + ocean_import)).astype(jnp.bfloat16)
    ocean_rows = (back_src_dev[:, 0] * OCN_DEV + back_src_tile).astype(jnp.int32)
    back_part = block_products(response[ocean_rows], back_blocks)
    atm_rows = (owner_dev * ATM_DEV + back_dst_tile).astype(jnp.int32)
    atm_import = jax.ops.segment_sum(back_part, atm_rows, num_segments=ATM_TILES)
    return ocean_import, atm_import
```

```python
import functools

import jax
import jax.numpy as jnp
from jax import lax
from jax.experimental import pallas as pl
from jax.experimental.pallas import tpu as pltpu
from jax.sharding import PartitionSpec as P

CHUNKS = 8
UNROLL = 8


def neighbour_ids(n_atmos, n_ocean):
    row, col = lax.axis_index("atm"), lax.axis_index("ocn")
    rows = [lax.rem(row + step + n_atmos, n_atmos) for step in (-1, 0, 1)]
    cols = [lax.rem(col + step + n_ocean, n_ocean) for step in (-1, 0, 1)]
    return [r * n_ocean + c for r in rows for c in cols]


def fill_table(table, n_atmos, n_ocean):
    for place, device in enumerate(neighbour_ids(n_atmos, n_ocean)):
        table[device] = place


def block_sums(blocks, source_of, target_of, load, total, chunk):
    def group(first, carry):
        at = first * UNROLL
        products = []
        for step in range(UNROLL):
            products.append(
                jnp.dot(load(source_of(at + step)), blocks[at + step], preferred_element_type=jnp.float32)
            )
        for step in range(UNROLL):
            target = target_of(at + step)
            total[target] = total[target] + products[step]
        return carry

    lax.fori_loop(chunk[0] // UNROLL, chunk[1] // UNROLL, group, 0)


def start_all(copies):
    for copy in copies:
        copy.start()
    return copies


def weight_copies(hbm, vmem, sems):
    count = hbm.shape[0] // CHUNKS
    return [
        pltpu.make_async_copy(
            hbm.at[pl.ds(c * count, count)], vmem.at[pl.ds(c * count, count)], sems.at[c]
        )
        for c in range(CHUNKS)
    ]


def fwd_kernel(
    n_atmos, n_ocean, fields_hbm, blocks_hbm, src_hbm, dev_hbm, tile_hbm, total,
    blocks, fields, src, dev, tile, table, sems, index_sems,
):
    tiles = total.shape[0] // 9
    small = start_all([
        pltpu.make_async_copy(src_hbm, src, index_sems.at[0]),
        pltpu.make_async_copy(dev_hbm, dev, index_sems.at[1]),
        pltpu.make_async_copy(tile_hbm, tile, index_sems.at[2]),
        pltpu.make_async_copy(fields_hbm, fields, index_sems.at[3]),
    ])
    weights = start_all(weight_copies(blocks_hbm, blocks, sems))
    fill_table(table, n_atmos, n_ocean)
    total[...] = jnp.zeros_like(total)
    for copy in small:
        copy.wait()
    count = blocks.shape[0] // CHUNKS
    for c in range(CHUNKS):
        weights[c].wait()
        block_sums(
            blocks, lambda b: src[b], lambda b: table[dev[b]] * tiles + tile[b],
            lambda s: fields[s], total, (c * count, (c + 1) * count),
        )


def bwd_kernel(
    n_atmos, n_ocean, near_ref, blocks, dev_hbm, src_hbm, dst_hbm, total,
    dev, src, dst, table, index_sems,
):
    tiles = near_ref.shape[0] // 9
    small = start_all([
        pltpu.make_async_copy(src_hbm, src, index_sems.at[0]),
        pltpu.make_async_copy(dev_hbm, dev, index_sems.at[1]),
        pltpu.make_async_copy(dst_hbm, dst, index_sems.at[2]),
    ])
    fill_table(table, n_atmos, n_ocean)
    total[...] = jnp.zeros_like(total)
    for copy in small:
        copy.wait()
    block_sums(
        blocks, lambda b: table[dev[b]] * tiles + src[b], lambda b: dst[b],
        lambda s: near_ref[s], total, (0, blocks.shape[0]),
    )


def in_hbm(*arrays):
    return [pltpu.with_memory_space_constraint(a, pltpu.HBM) for a in arrays]


def hbm():
    return pl.BlockSpec(memory_space=pl.ANY)


def vmem():
    return pl.BlockSpec(memory_space=pltpu.VMEM)


def forward(n_atmos, n_ocean, atm_fields, fwd_blocks, src, dev, tile, ocean_count):
    fields, cells = atm_fields.shape[1:]
    count = fwd_blocks.shape[0]
    return pl.pallas_call(
        functools.partial(fwd_kernel, n_atmos, n_ocean),
        out_shape=jax.ShapeDtypeStruct((9 * ocean_count, fields, cells), jnp.float32),
        in_specs=[hbm()] * 5,
        out_specs=vmem(),
        scratch_shapes=[
            pltpu.VMEM(fwd_blocks.shape, fwd_blocks.dtype),
            pltpu.VMEM(atm_fields.shape, atm_fields.dtype),
            pltpu.SMEM((count,), jnp.int32),
            pltpu.SMEM((count,), jnp.int32),
            pltpu.SMEM((count,), jnp.int32),
            pltpu.SMEM((n_atmos * n_ocean,), jnp.int32),
            pltpu.SemaphoreType.DMA((CHUNKS,)),
            pltpu.SemaphoreType.DMA((4,)),
        ],
        compiler_params=pltpu.CompilerParams(vmem_limit_bytes=16 * 2**20),
        name="forward_blocks",
    )(*in_hbm(atm_fields, fwd_blocks, src, dev, tile))


def backward(n_atmos, n_ocean, near, back_blocks, dev, src, dst, atmos_count):
    fields, cells = near.shape[1:]
    count = back_blocks.shape[0]
    return pl.pallas_call(
        functools.partial(bwd_kernel, n_atmos, n_ocean),
        out_shape=jax.ShapeDtypeStruct((atmos_count, fields, cells), jnp.float32),
        in_specs=[vmem()] * 2 + [hbm()] * 3,
        out_specs=vmem(),
        scratch_shapes=[
            pltpu.SMEM((count,), jnp.int32),
            pltpu.SMEM((count,), jnp.int32),
            pltpu.SMEM((count,), jnp.int32),
            pltpu.SMEM((n_atmos * n_ocean,), jnp.int32),
            pltpu.SemaphoreType.DMA((3,)),
        ],
        compiler_params=pltpu.CompilerParams(vmem_limit_bytes=16 * 2**20),
        name="backward_blocks",
    )(near, back_blocks, dev, src, dst)


def shift(block, axis, step):
    count = lax.axis_size(axis)
    return lax.ppermute(block, axis, [(i, (i + step) % count) for i in range(count)])


def gathered_sums(totals):
    for axis in ("ocn", "atm"):
        dim = totals.ndim - 4
        low, own, high = (lax.index_in_dim(totals, i, dim, keepdims=False) for i in range(3))
        from_high = shift(low.astype(jnp.float16), axis, -1)
        from_low = shift(high.astype(jnp.float16), axis, 1)
        totals = own + from_high.astype(jnp.float32) + from_low.astype(jnp.float32)
    return totals


def shards(
    atm_fields, fwd_blocks, fwd_src_tile, fwd_dst_dev, fwd_dst_tile, ocean_state, wet_mask,
    back_blocks, back_src_dev, back_src_tile, back_dst_tile,
):
    n_atmos = lax.axis_size("atm")
    n_ocean = lax.axis_size("ocn")
    fields, cells = atm_fields.shape[1:]
    ocean_count = ocean_state.shape[0]
    atmos_count = atm_fields.shape[0]
    totals = forward(
        n_atmos, n_ocean, atm_fields, fwd_blocks, fwd_src_tile, fwd_dst_dev[:, 0], fwd_dst_tile, ocean_count
    ).reshape(3, 3, ocean_count, fields, cells)
    ocean_import = gathered_sums(totals)
    wet = wet_mask.astype(jnp.float32)[:, None, :]
    response = (wet * jnp.tanh(ocean_state + ocean_import)).astype(jnp.bfloat16)
    near = response
    for axis in ("atm", "ocn"):
        low, high = shift(near, axis, 1), shift(near, axis, -1)
        near = jnp.stack([low, near, high], axis=0)
    near = jnp.swapaxes(near, 0, 1).reshape(9 * ocean_count, fields, cells)
    atm_import = backward(
        n_atmos, n_ocean, near, back_blocks, back_src_dev[:, 0], back_src_tile, back_dst_tile, atmos_count
    )
    return (ocean_import, atm_import)


def solution(mesh):
    part = ("atm", "ocn")
    three, two, one = P(part, None, None), P(part, None), P(part)
    in_specs = (three, three, one, two, one, three, two, three, two, one, one)
    return jax.shard_map(shards, mesh=mesh, in_specs=in_specs, out_specs=(three, three), check_vma=False)
```

```python
import functools

import jax
import jax.numpy as jnp
from jax import lax
from jax.experimental import pallas as pl
from jax.experimental.pallas import tpu as pltpu
from jax.sharding import PartitionSpec as P


CHUNKS = 4
UNROLL = 48
GROUP = 4
F32 = jnp.float32
F16 = jnp.float16
FIRST_SCALE = 8.0
SECOND_SCALE = 2.0


def neighbour_ids(n_atmos, n_ocean):
    row, col = lax.axis_index("atm"), lax.axis_index("ocn")
    rows = [lax.rem(row + step + n_atmos, n_atmos) for step in (-1, 0, 1)]
    cols = [lax.rem(col + step + n_ocean, n_ocean) for step in (-1, 0, 1)]
    return [r * n_ocean + c for r in rows for c in cols]


def fill_table(table, n_atmos, n_ocean):
    for place, device in enumerate(neighbour_ids(n_atmos, n_ocean)):
        table[device] = place


def stacked(first, second):
    spare = jnp.zeros((-first.shape[0] % 16, first.shape[1]), first.dtype)
    first = jnp.concatenate([first, spare], axis=0)
    second = jnp.concatenate([second, spare], axis=0)
    empty = jnp.zeros_like(first)
    return jnp.concatenate(
        [jnp.concatenate([first, empty], axis=1), jnp.concatenate([empty, second], axis=1)], axis=0
    )


def add_group(total, targets, products):
    sums = []
    for k, target in enumerate(targets):
        value = products[k]
        for j in range(k):
            value = value + jnp.where(targets[j] == target, products[j], 0.0)
        sums.append(total[target] + value)
    for target, value in zip(targets, sums):
        total[target] = value


def block_sums(blocks, source_of, target_of, load, total, begin, end):
    rows, cells = total.shape[1:]
    pairs = blocks.reshape(blocks.shape[0] // 2, 2 * cells, cells)

    def run(first, carry):
        at = first * UNROLL
        for group in range(0, UNROLL, GROUP):
            products = []
            for step in range(group, group + GROUP, 2):
                sources = stacked(load(source_of(at + step)), load(source_of(at + step + 1)))
                product = jnp.dot(sources, pairs[(at + step) // 2], preferred_element_type=F32)
                half = product.shape[0] // 2
                products += [product[:rows], product[half : half + rows]]
            add_group(total, [target_of(at + step) for step in range(group, group + GROUP)], products)
        return carry

    lax.fori_loop(begin // UNROLL, end // UNROLL, run, 0)


def start_all(copies):
    for copy in copies:
        copy.start()
    return copies


def fwd_kernel(
    n_atmos, n_ocean, fields_hbm, blocks_hbm, src_hbm, dev_hbm, tile_hbm, state_hbm, mask_hbm,
    own, low, high, surface, blocks, fields, total, mask, src, dev, tile, table, sems, index_sems,
):
    tiles = own.shape[1]
    rows = fields.shape[1]
    small = start_all([
        pltpu.make_async_copy(src_hbm, src, index_sems.at[0]),
        pltpu.make_async_copy(dev_hbm, dev, index_sems.at[1]),
        pltpu.make_async_copy(tile_hbm, tile, index_sems.at[2]),
        pltpu.make_async_copy(fields_hbm, fields, index_sems.at[3]),
    ])
    count = blocks.shape[0] // CHUNKS
    weights = start_all([
        pltpu.make_async_copy(
            blocks_hbm.at[pl.ds(c * count, count)], blocks.at[pl.ds(c * count, count)], sems.at[c]
        )
        for c in range(CHUNKS)
    ])
    late = start_all([
        pltpu.make_async_copy(state_hbm, surface.at[:, pl.ds(0, rows), :], index_sems.at[4]),
        pltpu.make_async_copy(mask_hbm, mask, index_sems.at[5]),
    ])
    fill_table(table, n_atmos, n_ocean)
    total[...] = jnp.zeros_like(total)
    for copy in small:
        copy.wait()
    for c in range(CHUNKS):
        weights[c].wait()
        block_sums(
            blocks, lambda b: src[b], lambda b: table[dev[b]] * tiles + tile[b],
            lambda s: fields[s], total, c * count, (c + 1) * count,
        )
    for row in range(3):
        for col, out in enumerate((low, own, high)):
            first = (row * 3 + col) * tiles
            part = total[first : first + tiles]
            out[row] = part
    for copy in late:
        copy.wait()
    wet = mask[...].astype(F32)
    surface[:, rows:, :] = jnp.broadcast_to(wet[:, None, :], (tiles, surface.shape[1] - rows, wet.shape[1]))


def bwd_kernel(n_atmos, n_ocean, near_ref, blocks, dev_hbm, src_hbm, dst_hbm, total, dev, src, dst, table, index_sems):
    tiles = near_ref.shape[0] // 9
    small = start_all([
        pltpu.make_async_copy(src_hbm, src, index_sems.at[0]),
        pltpu.make_async_copy(dev_hbm, dev, index_sems.at[1]),
        pltpu.make_async_copy(dst_hbm, dst, index_sems.at[2]),
    ])
    fill_table(table, n_atmos, n_ocean)
    total[...] = jnp.zeros_like(total)
    for copy in small:
        copy.wait()
    block_sums(
        blocks, lambda b: table[dev[b]] * tiles + src[b], lambda b: dst[b],
        lambda s: near_ref[s], total, 0, blocks.shape[0],
    )


def in_hbm(*arrays):
    return [pltpu.with_memory_space_constraint(a, pltpu.HBM) for a in arrays]


def hbm():
    return pl.BlockSpec(memory_space=pl.ANY)


def vmem():
    return pl.BlockSpec(memory_space=pltpu.VMEM)


def forward(n_atmos, n_ocean, atm_fields, fwd_blocks, src, dev, tile, state, mask):
    fields, cells = atm_fields.shape[1:]
    count = fwd_blocks.shape[0]
    tiles = state.shape[0]
    index = pltpu.SMEM((count,), jnp.int32)
    part = (3, tiles, fields, cells)
    return pl.pallas_call(
        functools.partial(fwd_kernel, n_atmos, n_ocean),
        out_shape=[
            jax.ShapeDtypeStruct(part, F32),
            jax.ShapeDtypeStruct(part, F32),
            jax.ShapeDtypeStruct(part, F32),
            jax.ShapeDtypeStruct((tiles, fields + 8, cells), F32),
        ],
        in_specs=[hbm()] * 7,
        out_specs=[vmem()] * 4,
        scratch_shapes=[
            pltpu.VMEM(fwd_blocks.shape, fwd_blocks.dtype),
            pltpu.VMEM(atm_fields.shape, atm_fields.dtype),
            pltpu.VMEM((9 * tiles, fields, cells), F32),
            pltpu.VMEM(mask.shape, mask.dtype),
            index, index, index,
            pltpu.SMEM((n_atmos * n_ocean,), jnp.int32),
            pltpu.SemaphoreType.DMA((CHUNKS,)),
            pltpu.SemaphoreType.DMA((6,)),
        ],
        compiler_params=pltpu.CompilerParams(vmem_limit_bytes=16 * 2**20),
        name="forward_blocks",
    )(*in_hbm(atm_fields, fwd_blocks, src, dev, tile, state, mask))


def backward(n_atmos, n_ocean, near, back_blocks, dev, src, dst, atmos_count):
    fields, cells = near.shape[1:]
    count = back_blocks.shape[0]
    index = pltpu.SMEM((count,), jnp.int32)
    return pl.pallas_call(
        functools.partial(bwd_kernel, n_atmos, n_ocean),
        out_shape=jax.ShapeDtypeStruct((atmos_count, fields, cells), F32),
        in_specs=[vmem()] * 2 + [hbm()] * 3,
        out_specs=vmem(),
        scratch_shapes=[
            index, index, index,
            pltpu.SMEM((n_atmos * n_ocean,), jnp.int32),
            pltpu.SemaphoreType.DMA((3,)),
        ],
        compiler_params=pltpu.CompilerParams(vmem_limit_bytes=16 * 2**20),
        name="backward_blocks",
    )(near, back_blocks, dev, src, dst)


def shift(block, axis, step):
    count = lax.axis_size(axis)
    return lax.ppermute(block, axis, [(i, (i + step) % count) for i in range(count)])


def swap(low, high, axis, step=1):
    from_upper = shift(low, axis, -step)
    from_lower = shift(high, axis, step)
    return from_upper, from_lower


def shards(
    atm_fields, fwd_blocks, fwd_src_tile, fwd_dst_dev, fwd_dst_tile, ocean_state, wet_mask,
    back_blocks, back_src_dev, back_src_tile, back_dst_tile,
):
    n_atmos = lax.axis_size("atm")
    n_ocean = lax.axis_size("ocn")
    fields, cells = atm_fields.shape[1:]
    ocean_count = ocean_state.shape[0]
    atmos_count = atm_fields.shape[0]
    own, low, high, surface = forward(
        n_atmos, n_ocean, atm_fields, fwd_blocks, fwd_src_tile, fwd_dst_dev[:, 0], fwd_dst_tile, ocean_state, wet_mask
    )
    upper, lower = swap((low * FIRST_SCALE).astype(F16), (high * FIRST_SCALE).astype(F16), "ocn")
    above, below = swap(surface, surface, "atm")
    surface = jnp.stack([below, surface, above])
    row_sums = own + (upper.astype(F32) + lower.astype(F32)) * (1.0 / FIRST_SCALE)
    sent = (row_sums * SECOND_SCALE).astype(F16)
    from_above, from_below = swap(sent[:2], sent[1:], "atm")
    from_two_above, from_two_below = swap(sent[0], sent[2], "atm", 2)
    near_sums = jnp.stack([from_below[0], from_below[1], from_above[1]]).astype(F32)
    far_sums = jnp.stack([from_two_below, from_above[0], from_two_above]).astype(F32)
    sums = row_sums + (near_sums + far_sums) * (1.0 / SECOND_SCALE)
    wet = surface[:, :, fields : fields + 1]
    response = (wet * jnp.tanh(surface[:, :, :fields] + sums)).astype(jnp.bfloat16)
    upper, lower = swap(response, response, "ocn")
    near = jnp.stack([lower, response, upper], axis=1).reshape(9 * ocean_count, fields, cells)
    atm_import = backward(
        n_atmos, n_ocean, near, back_blocks, back_src_dev[:, 0], back_src_tile, back_dst_tile, atmos_count
    )
    return (sums[1], atm_import)


def solution(mesh):
    part = ("atm", "ocn")
    three, two, one = P(part, None, None), P(part, None), P(part)
    in_specs = (three, three, one, two, one, three, two, three, two, one, one)
    return jax.shard_map(shards, mesh=mesh, in_specs=in_specs, out_specs=(three, three), check_vma=False)
```

```python
import functools

import jax
import jax.numpy as jnp
from jax import lax
from jax.experimental import pallas as pl
from jax.experimental.pallas import tpu as pltpu
from jax.sharding import PartitionSpec as P


CHUNKS = 4
GROUP = 4
F32 = jnp.float32
F16 = jnp.float16
FIRST_SCALE = 8.0
SECOND_SCALE = 2.0


def partner_step(axis):
    return 1 - 2 * (lax.axis_index(axis) % 2)


def near_places(device, n_atmos, n_ocean):
    row, col = lax.axis_index("atm"), lax.axis_index("ocn")
    row_side, col_side = partner_step("atm"), partner_step("ocn")
    place = jnp.zeros_like(device)
    for i, row_step in enumerate((-row_side, 0, row_side)):
        for j, col_step in enumerate((-col_side, 0, col_side)):
            name = (row + row_step + n_atmos) % n_atmos * n_ocean + (col + col_step + n_ocean) % n_ocean
            place = jnp.where(device == name, 3 * i + j, place)
    return place


def stacked(first, second):
    spare = jnp.zeros((-first.shape[0] % 16, first.shape[1]), first.dtype)
    first = jnp.concatenate([first, spare], axis=0)
    second = jnp.concatenate([second, spare], axis=0)
    empty = jnp.zeros_like(first)
    return jnp.concatenate(
        [jnp.concatenate([first, empty], axis=1), jnp.concatenate([empty, second], axis=1)], axis=0
    )


def add_group(total, rows, targets, products):
    places = [pl.ds(pl.multiple_of(target, 8), rows) for target in targets]
    sums = []
    for k, target in enumerate(targets):
        value = products[k]
        for j in range(k):
            value = value + jnp.where(targets[j] == target, products[j], 0.0)
        sums.append(total[places[k], :] + value)
    for place, value in zip(places, sums):
        total[place, :] = value


def block_sums(blocks, source_of, target_of, load, total, rows, begin, end):
    cells = total.shape[1]
    pairs = blocks.reshape(blocks.shape[0] // 2, 2 * cells, cells)
    for group in range(begin, end, GROUP):
        products = []
        for at in range(group, group + GROUP, 2):
            sources = stacked(load(source_of(at)), load(source_of(at + 1)))
            product = jnp.dot(sources, pairs[at // 2], preferred_element_type=F32)
            half = product.shape[0] // 2
            products += [product[:rows], product[half : half + rows]]
        add_group(total, rows, [target_of(at) for at in range(group, group + GROUP)], products)


def start_all(*copies):
    for copy in copies:
        copy.start()
    return copies


def fwd_kernel(
    n_atmos, n_ocean, fields_hbm, blocks_hbm, src_hbm, dev_hbm, tile_hbm, state_hbm, mask_hbm,
    back_dev_hbm, back_src_hbm, back_dst_hbm,
    own, outer_col, inner_col, surface, back_index, same_side,
    blocks, fields, total, mask, dev_v, tile_v, place_v, back_v, src, place, sems, index_sems,
):
    tiles = own.shape[1]
    rows = fields.shape[1]
    index = start_all(
        pltpu.make_async_copy(dev_hbm, dev_v, index_sems.at[0]),
        pltpu.make_async_copy(tile_hbm, tile_v, index_sems.at[1]),
        pltpu.make_async_copy(src_hbm, src, index_sems.at[2]),
    )
    source = start_all(pltpu.make_async_copy(fields_hbm, fields, index_sems.at[3]))
    count = blocks.shape[0] // CHUNKS
    weights = start_all(*[
        pltpu.make_async_copy(
            blocks_hbm.at[pl.ds(c * count, count)], blocks.at[pl.ds(c * count, count)], sems.at[c]
        )
        for c in range(CHUNKS)
    ])
    late = start_all(
        pltpu.make_async_copy(state_hbm, surface.at[:, pl.ds(0, rows), :], index_sems.at[4]),
        pltpu.make_async_copy(mask_hbm, mask, index_sems.at[5]),
        pltpu.make_async_copy(back_dev_hbm, back_v.at[0], index_sems.at[6]),
        pltpu.make_async_copy(back_src_hbm, back_v.at[1], index_sems.at[7]),
        pltpu.make_async_copy(back_dst_hbm, back_v.at[2], index_sems.at[8]),
    )
    total[...] = jnp.zeros_like(total)
    for copy in index[:2]:
        copy.wait()
    place_v[...] = (near_places(dev_v[...], n_atmos, n_ocean) * tiles + tile_v[...]) * rows
    to_scalars = start_all(pltpu.make_async_copy(place_v, place, index_sems.at[0]))
    for copy in to_scalars + index[2:] + source:
        copy.wait()
    for c in range(CHUNKS):
        weights[c].wait()
        block_sums(
            blocks, lambda b: src[0, b], lambda b: place[0, b], lambda s: fields[s],
            total, rows, c * count, (c + 1) * count,
        )
    for row in range(3):
        for col, out in enumerate((outer_col, own, inner_col)):
            first = (row * 3 + col) * tiles * rows
            out[row] = total[first : first + tiles * rows, :].reshape(out.shape[1:])
    for copy in late:
        copy.wait()
    wet = mask[...].astype(F32)
    surface[:, rows:, :] = jnp.broadcast_to(wet[:, None, :], (tiles, surface.shape[1] - rows, wet.shape[1]))
    back_index[0] = near_places(back_v[0], n_atmos, n_ocean) * tiles + back_v[1]
    back_index[1] = back_v[2] * rows
    row = lax.axis_index("atm")
    same_side[...] = jnp.full_like(same_side, jnp.where(row % 2 == row // 2 % 2, 1, 0))


def bwd_kernel(near, blocks, index_in, out, total, index, sems):
    rows = near.shape[1]
    copies = start_all(pltpu.make_async_copy(index_in, index, sems.at[0]))
    total[...] = jnp.zeros_like(total)
    for copy in copies:
        copy.wait()
    block_sums(
        blocks, lambda b: index[0, 0, b], lambda b: index[1, 0, b], lambda s: near[s],
        total, rows, 0, blocks.shape[0],
    )
    result = pltpu.make_async_copy(total, out, sems.at[0])
    result.start()
    result.wait()


def in_hbm(*arrays):
    return [pltpu.with_memory_space_constraint(a, pltpu.HBM) for a in arrays]


def hbm():
    return pl.BlockSpec(memory_space=pl.ANY)


def vmem():
    return pl.BlockSpec(memory_space=pltpu.VMEM)


def forward(n_atmos, n_ocean, atm_fields, fwd_blocks, index, state, mask, back_index):
    fields, cells = atm_fields.shape[1:]
    count = fwd_blocks.shape[0]
    tiles = state.shape[0]
    part = (3, tiles, fields, cells)
    numbers = pltpu.VMEM((1, count), jnp.int32)
    scalars = pltpu.SMEM((1, count), jnp.int32)
    return pl.pallas_call(
        functools.partial(fwd_kernel, n_atmos, n_ocean),
        out_shape=[
            jax.ShapeDtypeStruct(part, F32),
            jax.ShapeDtypeStruct(part, F32),
            jax.ShapeDtypeStruct(part, F32),
            jax.ShapeDtypeStruct((tiles, fields + 8, cells), F32),
            jax.ShapeDtypeStruct((2, 1, count), jnp.int32),
            jax.ShapeDtypeStruct((1, 1, cells), jnp.int32),
        ],
        in_specs=[hbm()] * 10,
        out_specs=[vmem()] * 6,
        scratch_shapes=[
            pltpu.VMEM(fwd_blocks.shape, fwd_blocks.dtype),
            pltpu.VMEM(atm_fields.shape, atm_fields.dtype),
            pltpu.VMEM((9 * tiles * fields, cells), F32),
            pltpu.VMEM(mask.shape, mask.dtype),
            numbers, numbers, numbers,
            pltpu.VMEM((3, 1, count), jnp.int32),
            scalars, scalars,
            pltpu.SemaphoreType.DMA((CHUNKS,)),
            pltpu.SemaphoreType.DMA((9,)),
        ],
        compiler_params=pltpu.CompilerParams(vmem_limit_bytes=10 * 2**20),
        name="forward_blocks",
    )(*in_hbm(atm_fields, fwd_blocks, *index, state, mask, *back_index))


def backward(near, back_blocks, index, atmos_count):
    fields, cells = near.shape[1:]
    return pl.pallas_call(
        bwd_kernel,
        out_shape=jax.ShapeDtypeStruct((atmos_count * fields, cells), F32),
        in_specs=[vmem()] * 3,
        out_specs=hbm(),
        scratch_shapes=[
            pltpu.VMEM((atmos_count * fields, cells), F32),
            pltpu.SMEM(index.shape, jnp.int32),
            pltpu.SemaphoreType.DMA((1,)),
        ],
        compiler_params=pltpu.CompilerParams(vmem_limit_bytes=4 * 2**20),
        name="backward_blocks",
    )(near, back_blocks, index).reshape(atmos_count, fields, cells)


def ring_pairs(count, stride, inner):
    pairs = []
    for i in range(count):
        step = stride if (i // stride % 2 == 0) == inner else -stride
        pairs.append((i, (i + step) % count))
    return pairs


def swap(block, axis, stride, inner):
    return lax.ppermute(block, axis, ring_pairs(lax.axis_size(axis), stride, inner))


def shards(
    atm_fields, fwd_blocks, fwd_src_tile, fwd_dst_dev, fwd_dst_tile, ocean_state, wet_mask,
    back_blocks, back_src_dev, back_src_tile, back_dst_tile,
):
    n_atmos = lax.axis_size("atm")
    n_ocean = lax.axis_size("ocn")
    fields, cells = atm_fields.shape[1:]
    ocean_count = ocean_state.shape[0]
    atmos_count = atm_fields.shape[0]
    flat = (1, fwd_src_tile.shape[0])
    own, outer_col, inner_col, surface, index, same_side = forward(
        n_atmos, n_ocean, atm_fields, fwd_blocks,
        [a.reshape(flat) for a in (fwd_src_tile, fwd_dst_dev, fwd_dst_tile)],
        ocean_state, wet_mask,
        [a.reshape(flat) for a in (back_src_dev, back_src_tile, back_dst_tile)],
    )
    from_inner = swap((inner_col * FIRST_SCALE).astype(F16), "ocn", 1, True)
    from_outer = swap((outer_col * FIRST_SCALE).astype(F16), "ocn", 1, False)
    row_sums = own + (from_inner.astype(F32) + from_outer.astype(F32)) * (1.0 / FIRST_SCALE)
    sent = (row_sums * SECOND_SCALE).astype(F16)
    same = same_side > 0
    to_inner = jnp.where(same, sent[2], sent[0])
    to_outer = jnp.where(same, sent[0], sent[2])
    inner_state = swap(surface, "atm", 1, True)
    outer_state = swap(surface, "atm", 1, False)
    inner = swap(sent[1:], "atm", 1, True)
    outer = swap(sent[:2], "atm", 1, False)
    far_inner = swap(to_inner, "atm", 2, True)
    far_outer = swap(to_outer, "atm", 2, False)
    direct = jnp.stack([outer[1], inner[1], inner[0]]).astype(F32)
    other = jnp.stack([jnp.where(same, far_outer, far_inner), outer[0], jnp.where(same, far_inner, far_outer)]).astype(F32)
    sums = row_sums + (direct + other) * (1.0 / SECOND_SCALE)
    surface = jnp.stack([outer_state, surface, inner_state])
    wet = surface[:, :, fields : fields + 1]
    response = (wet * jnp.tanh(surface[:, :, :fields] + sums)).astype(jnp.bfloat16)
    inner_near = swap(response, "ocn", 1, True)
    outer_near = swap(response, "ocn", 1, False)
    near = jnp.stack([outer_near, response, inner_near], axis=1).reshape(9 * ocean_count, fields, cells)
    return (sums[1], backward(near, back_blocks, index, atmos_count))


def solution(mesh):
    part = ("atm", "ocn")
    three, two, one = P(part, None, None), P(part, None), P(part)
    in_specs = (three, three, one, two, one, three, two, three, two, one, one)
    return jax.shard_map(shards, mesh=mesh, in_specs=in_specs, out_specs=(three, three), check_vma=False)
```

```python
import functools

import jax
import jax.numpy as jnp
from jax import lax
from jax.experimental import pallas as pl
from jax.experimental.pallas import tpu as pltpu
from jax.sharding import PartitionSpec as P


CHUNKS = 4
GROUP = 4
F32 = jnp.float32
F16 = jnp.float16
FIRST_SCALE = 8.0
SECOND_SCALE = 2.0


def partner_step(axis):
    return 1 - 2 * (lax.axis_index(axis) % 2)


def near_places(device, n_atmos, n_ocean):
    row, col = lax.axis_index("atm"), lax.axis_index("ocn")
    row_side, col_side = partner_step("atm"), partner_step("ocn")
    place = jnp.zeros_like(device)
    for i, row_step in enumerate((-row_side, 0, row_side)):
        for j, col_step in enumerate((-col_side, 0, col_side)):
            name = (row + row_step + n_atmos) % n_atmos * n_ocean + (col + col_step + n_ocean) % n_ocean
            place = jnp.where(device == name, 3 * j + i, place)
    return place


def stacked(first, second):
    spare = jnp.zeros((-first.shape[0] % 16, first.shape[1]), first.dtype)
    first = jnp.concatenate([first, spare], axis=0)
    second = jnp.concatenate([second, spare], axis=0)
    empty = jnp.zeros_like(first)
    return jnp.concatenate(
        [jnp.concatenate([first, empty], axis=1), jnp.concatenate([empty, second], axis=1)], axis=0
    )


def add_group(total, rows, targets, products):
    places = [pl.ds(pl.multiple_of(target, 8), rows) for target in targets]
    sums = []
    for k, target in enumerate(targets):
        value = products[k]
        for j in range(k):
            value = value + jnp.where(targets[j] == target, products[j], 0.0)
        sums.append(total[places[k], :] + value)
    for place, value in zip(places, sums):
        total[place, :] = value


def block_sums(begin, end, block_of, weights, load, source_of, target_of, total, rows):
    for group in range(0, end, GROUP):
        numbers = [block_of(begin + at) for at in range(group, group + GROUP)]
        products = []
        for first, second in zip(numbers[::2], numbers[1::2]):
            sources = stacked(load(source_of(first)), load(source_of(second)))
            pair = weights(first, second)
            product = jnp.dot(sources, pair, preferred_element_type=F32)
            half = product.shape[0] // 2
            products += [product[:rows], product[half : half + rows]]
        add_group(total, rows, [target_of(number) for number in numbers], products)


def start_all(*copies):
    for copy in copies:
        copy.start()
    return copies


def fwd_kernel(
    n_atmos, n_ocean, fields_hbm, blocks_hbm, src_hbm, dev_hbm, tile_hbm, state_hbm, mask_hbm,
    back_dev_hbm, back_src_hbm, back_dst_hbm,
    total, surface, back_index, same_side,
    blocks, fields, mask, dev_v, tile_v, place_v, back_v, src, place, sems, index_sems,
):
    tiles = mask.shape[0]
    rows = fields.shape[1]
    index = start_all(
        pltpu.make_async_copy(dev_hbm, dev_v, index_sems.at[0]),
        pltpu.make_async_copy(tile_hbm, tile_v, index_sems.at[1]),
        pltpu.make_async_copy(src_hbm, src, index_sems.at[2]),
    )
    source = start_all(pltpu.make_async_copy(fields_hbm, fields, index_sems.at[3]))
    count = blocks.shape[0] // CHUNKS
    weights = start_all(*[
        pltpu.make_async_copy(
            blocks_hbm.at[pl.ds(c * count, count)], blocks.at[pl.ds(c * count, count)], sems.at[c]
        )
        for c in range(CHUNKS)
    ])
    late = start_all(
        pltpu.make_async_copy(state_hbm, surface.at[pl.ds(0, tiles * rows), :], index_sems.at[4]),
        pltpu.make_async_copy(mask_hbm, mask, index_sems.at[5]),
        pltpu.make_async_copy(back_dev_hbm, back_v.at[0], index_sems.at[6]),
        pltpu.make_async_copy(back_src_hbm, back_v.at[1], index_sems.at[7]),
        pltpu.make_async_copy(back_dst_hbm, back_v.at[2], index_sems.at[8]),
    )
    total[...] = jnp.zeros_like(total)
    for copy in index[:2]:
        copy.wait()
    place_v[...] = (near_places(dev_v[...], n_atmos, n_ocean) * tiles + tile_v[...]) * rows
    to_scalars = start_all(pltpu.make_async_copy(place_v, place, index_sems.at[0]))
    for copy in to_scalars + index[2:] + source:
        copy.wait()
    pairs = blocks.reshape(blocks.shape[0] // 2, 2 * blocks.shape[1], blocks.shape[2])
    for c in range(CHUNKS):
        weights[c].wait()
        block_sums(
            c * count, count, lambda b: b, lambda b, _: pairs[b // 2], lambda s: fields[s],
            lambda b: src[0, b], lambda b: place[0, b], total, rows,
        )
    for copy in late:
        copy.wait()
    surface[tiles * rows :, :] = mask[...].astype(F32)
    back_index[0] = near_places(back_v[0], n_atmos, n_ocean) * tiles + back_v[1]
    back_index[1] = back_v[2] * rows
    row = lax.axis_index("atm")
    same_side[...] = jnp.full_like(same_side, jnp.where(row % 2 == row // 2 % 2, 1, 0))


def run_step(count):
    return next(step for step in (48, 16, 8, 4) if count % step == 0)


def run_blocks(first, last, near, blocks, index, order, total, skipped):
    rows = near.shape[1]
    step = run_step(blocks.shape[0])

    def trip(at, carry):
        block_sums(
            at * step, step, lambda b: order[b],
            lambda b, c: jnp.concatenate([blocks[b], blocks[c]], axis=0), lambda s: near[s],
            lambda b: index[0, 0, b] - skipped, lambda b: index[1, 0, b], total, rows,
        )
        return carry

    lax.fori_loop(first, last, trip, 0)


def early_kernel(tiles, near, blocks, index_in, total, order_out, index, order, sems):
    count = blocks.shape[0]
    outer = 3 * tiles
    copy = pltpu.make_async_copy(index_in, index, sems.at[0])
    copy.start()
    total[...] = jnp.zeros_like(total)
    copy.wait()

    def place_block(b, ends):
        front, back = ends
        far = (index[0, 0, b] < outer).astype(jnp.int32)
        order[jnp.where(far == 1, back, front)] = b
        return front + 1 - far, back - far

    ready, _ = lax.fori_loop(0, count, place_block, (jnp.int32(0), jnp.int32(count - 1)), unroll=8)
    trips = ready // run_step(count)
    order[count] = trips
    copy = pltpu.make_async_copy(order, order_out, sems.at[0])
    copy.start()
    run_blocks(0, trips, near, blocks, index, order, total, outer)
    copy.wait()


def late_kernel(near, blocks, index_in, order_in, total_in, total, out, index, order, sems):
    count = blocks.shape[0]
    copies = start_all(
        pltpu.make_async_copy(index_in, index, sems.at[0]), pltpu.make_async_copy(order_in, order, sems.at[1])
    )
    for copy in copies:
        copy.wait()
    run_blocks(order[count], count // run_step(count), near, blocks, index, order, total, 0)
    result = pltpu.make_async_copy(total, out, sems.at[0])
    result.start()
    result.wait()


def in_hbm(*arrays):
    return [pltpu.with_memory_space_constraint(a, pltpu.HBM) for a in arrays]


def hbm():
    return pl.BlockSpec(memory_space=pl.ANY)


def vmem():
    return pl.BlockSpec(memory_space=pltpu.VMEM)


def forward(n_atmos, n_ocean, atm_fields, fwd_blocks, index, state, mask, back_index):
    fields, cells = atm_fields.shape[1:]
    count = fwd_blocks.shape[0]
    tiles = state.shape[0]
    numbers = pltpu.VMEM((1, count), jnp.int32)
    scalars = pltpu.SMEM((1, count), jnp.int32)
    return pl.pallas_call(
        functools.partial(fwd_kernel, n_atmos, n_ocean),
        out_shape=[
            jax.ShapeDtypeStruct((9 * tiles * fields, cells), F32),
            jax.ShapeDtypeStruct((tiles * fields + tiles, cells), F32),
            jax.ShapeDtypeStruct((2, 1, count), jnp.int32),
            jax.ShapeDtypeStruct((1, 1, cells), jnp.int32),
        ],
        in_specs=[hbm()] * 10,
        out_specs=[vmem()] * 4,
        scratch_shapes=[
            pltpu.VMEM(fwd_blocks.shape, fwd_blocks.dtype),
            pltpu.VMEM(atm_fields.shape, atm_fields.dtype),
            pltpu.VMEM(mask.shape, mask.dtype),
            numbers, numbers, numbers,
            pltpu.VMEM((3, 1, count), jnp.int32),
            scalars, scalars,
            pltpu.SemaphoreType.DMA((CHUNKS,)),
            pltpu.SemaphoreType.DMA((9,)),
        ],
        compiler_params=pltpu.CompilerParams(vmem_limit_bytes=10 * 2**20),
        name="forward_blocks",
    )(*in_hbm(atm_fields, fwd_blocks, *index, state.reshape(tiles * fields, cells), mask, *back_index))


def backward_early(near, back_blocks, index, tiles, atmos_count):
    fields, cells = near.shape[1:]
    count = back_blocks.shape[0]
    listed = (count + 64,)
    return pl.pallas_call(
        functools.partial(early_kernel, tiles),
        out_shape=[
            jax.ShapeDtypeStruct((atmos_count * fields, cells), F32),
            jax.ShapeDtypeStruct(listed, jnp.int32),
        ],
        in_specs=[vmem()] * 3,
        out_specs=[vmem(), vmem()],
        scratch_shapes=[
            pltpu.SMEM(index.shape, jnp.int32),
            pltpu.SMEM(listed, jnp.int32),
            pltpu.SemaphoreType.DMA((1,)),
        ],
        compiler_params=pltpu.CompilerParams(vmem_limit_bytes=4 * 2**20),
        name="early_blocks",
    )(near, back_blocks, index)


def backward_late(near, back_blocks, index, order, total):
    fields, cells = near.shape[1:]
    shape = jax.ShapeDtypeStruct(total.shape, F32)
    _, out = pl.pallas_call(
        late_kernel,
        out_shape=[shape, shape],
        in_specs=[vmem()] * 5,
        out_specs=[vmem(), hbm()],
        scratch_shapes=[
            pltpu.SMEM(index.shape, jnp.int32),
            pltpu.SMEM(order.shape, jnp.int32),
            pltpu.SemaphoreType.DMA((2,)),
        ],
        input_output_aliases={4: 0},
        compiler_params=pltpu.CompilerParams(vmem_limit_bytes=4 * 2**20),
        name="backward_blocks",
    )(near, back_blocks, index, order, total)
    return out.reshape(-1, fields, cells)


def ring_pairs(count, stride, inner):
    pairs = []
    for i in range(count):
        step = stride if (i // stride % 2 == 0) == inner else -stride
        pairs.append((i, (i + step) % count))
    return pairs


def swap(block, axis, stride, inner):
    return lax.ppermute(block, axis, ring_pairs(lax.axis_size(axis), stride, inner))


def shards(
    atm_fields, fwd_blocks, fwd_src_tile, fwd_dst_dev, fwd_dst_tile, ocean_state, wet_mask,
    back_blocks, back_src_dev, back_src_tile, back_dst_tile,
):
    n_atmos = lax.axis_size("atm")
    n_ocean = lax.axis_size("ocn")
    fields, cells = atm_fields.shape[1:]
    ocean_count = ocean_state.shape[0]
    atmos_count = atm_fields.shape[0]
    flat = (1, fwd_src_tile.shape[0])
    totals, surface, index, same_side = forward(
        n_atmos, n_ocean, atm_fields, fwd_blocks,
        [a.reshape(flat) for a in (fwd_src_tile, fwd_dst_dev, fwd_dst_tile)],
        ocean_state, wet_mask,
        [a.reshape(flat) for a in (back_src_dev, back_src_tile, back_dst_tile)],
    )
    outer_col, own, inner_col = totals.reshape(3, 3, ocean_count, fields, cells)
    from_inner = swap((inner_col * FIRST_SCALE).astype(F16), "ocn", 1, True)
    from_outer = swap((outer_col * FIRST_SCALE).astype(F16), "ocn", 1, False)
    row_sums = own + (from_inner.astype(F32) + from_outer.astype(F32)) * (1.0 / FIRST_SCALE)
    sent = (row_sums * SECOND_SCALE).astype(F16)
    same = same_side > 0
    to_inner = jnp.where(same, sent[2], sent[0])
    to_outer = jnp.where(same, sent[0], sent[2])
    inner_state = swap(surface, "atm", 1, True)
    outer_state = swap(surface, "atm", 1, False)
    inner = swap(sent[1:], "atm", 1, True)
    outer = swap(sent[:2], "atm", 1, False)
    far_inner = swap(to_inner, "atm", 2, True)
    far_outer = swap(to_outer, "atm", 2, False)
    direct = jnp.stack([outer[1], inner[1], inner[0]]).astype(F32)
    other = jnp.stack([jnp.where(same, far_outer, far_inner), outer[0], jnp.where(same, far_inner, far_outer)]).astype(F32)
    sums = row_sums + (direct + other) * (1.0 / SECOND_SCALE)
    surface = jnp.stack([outer_state, surface, inner_state])
    state = surface[:, : ocean_count * fields].reshape(sums.shape)
    wet = surface[:, ocean_count * fields :].reshape(3, ocean_count, 1, cells)
    response = (wet * jnp.tanh(state + sums)).astype(jnp.bfloat16)
    inner_near = swap(response, "ocn", 1, True)
    outer_near = swap(response, "ocn", 1, False)
    ready = jnp.stack([response, inner_near]).reshape(6 * ocean_count, fields, cells)
    total, order = backward_early(ready, back_blocks, index, ocean_count, atmos_count)
    near = jnp.stack([outer_near, response, inner_near]).reshape(9 * ocean_count, fields, cells)
    return (sums[1], backward_late(near, back_blocks, index, order, total))


def solution(mesh):
    part = ("atm", "ocn")
    three, two, one = P(part, None, None), P(part, None), P(part)
    in_specs = (three, three, one, two, one, three, two, three, two, one, one)
    return jax.shard_map(shards, mesh=mesh, in_specs=in_specs, out_specs=(three, three), check_vma=False)
```

```python
import functools

import jax
import jax.numpy as jnp
from jax import lax
from jax.experimental import pallas as pl
from jax.experimental.pallas import tpu as pltpu
from jax.sharding import PartitionSpec as P


CHUNKS = 4
GROUP = 4
F32 = jnp.float32
F16 = jnp.float16
FIRST_SCALE = 8.0
SECOND_SCALE = 2.0


def partner_step(axis):
    return 1 - 2 * (lax.axis_index(axis) % 2)


def near_places(device, n_atmos, n_ocean):
    row, col = lax.axis_index("atm"), lax.axis_index("ocn")
    row_side, col_side = partner_step("atm"), partner_step("ocn")
    place = jnp.zeros_like(device)
    for i, row_step in enumerate((-row_side, 0, row_side)):
        for j, col_step in enumerate((-col_side, 0, col_side)):
            name = (row + row_step + n_atmos) % n_atmos * n_ocean + (col + col_step + n_ocean) % n_ocean
            place = jnp.where(device == name, 3 * j + i, place)
    return place


def stacked(first, second):
    spare = jnp.zeros((-first.shape[0] % 16, first.shape[1]), first.dtype)
    first = jnp.concatenate([first, spare], axis=0)
    second = jnp.concatenate([second, spare], axis=0)
    empty = jnp.zeros_like(first)
    return jnp.concatenate(
        [jnp.concatenate([first, empty], axis=1), jnp.concatenate([empty, second], axis=1)], axis=0
    )


def add_group(total, rows, targets, products):
    places = [pl.ds(pl.multiple_of(target, 8), rows) for target in targets]
    sums = []
    for k, target in enumerate(targets):
        value = products[k]
        for j in range(k):
            value = value + jnp.where(targets[j] == target, products[j], 0.0)
        sums.append(total[places[k], :] + value)
    for place, value in zip(places, sums):
        total[place, :] = value


def block_sums(begin, end, block_of, weights, load, source_of, target_of, total, rows):
    for group in range(0, end, GROUP):
        numbers = [block_of(begin + at) for at in range(group, group + GROUP)]
        products = []
        for first, second in zip(numbers[::2], numbers[1::2]):
            sources = stacked(load(source_of(first)), load(source_of(second)))
            pair = weights(first, second)
            product = jnp.dot(sources, pair, preferred_element_type=F32)
            half = product.shape[0] // 2
            products += [product[:rows], product[half : half + rows]]
        add_group(total, rows, [target_of(number) for number in numbers], products)


def start_all(*copies):
    for copy in copies:
        copy.start()
    return copies


def fwd_kernel(
    n_atmos, n_ocean, fields_hbm, blocks_hbm, src_hbm, dev_hbm, tile_hbm, state_hbm, mask_hbm,
    back_dev_hbm, back_src_hbm, back_dst_hbm,
    total, surface, back_index, same_side,
    blocks, fields, mask, dev_v, tile_v, place_v, back_v, src, place, sems, index_sems,
):
    tiles = mask.shape[0]
    rows = fields.shape[1]
    index = start_all(
        pltpu.make_async_copy(dev_hbm, dev_v, index_sems.at[0]),
        pltpu.make_async_copy(tile_hbm, tile_v, index_sems.at[1]),
        pltpu.make_async_copy(src_hbm, src, index_sems.at[2]),
    )
    source = start_all(pltpu.make_async_copy(fields_hbm, fields, index_sems.at[3]))
    count = blocks.shape[0] // CHUNKS
    weights = start_all(*[
        pltpu.make_async_copy(
            blocks_hbm.at[pl.ds(c * count, count)], blocks.at[pl.ds(c * count, count)], sems.at[c]
        )
        for c in range(CHUNKS)
    ])
    late = start_all(
        pltpu.make_async_copy(state_hbm, surface.at[pl.ds(0, tiles * rows), :], index_sems.at[4]),
        pltpu.make_async_copy(mask_hbm, mask, index_sems.at[5]),
        pltpu.make_async_copy(back_dev_hbm, back_v.at[0], index_sems.at[6]),
        pltpu.make_async_copy(back_src_hbm, back_v.at[1], index_sems.at[7]),
        pltpu.make_async_copy(back_dst_hbm, back_v.at[2], index_sems.at[8]),
    )
    total[...] = jnp.zeros_like(total)
    for copy in index[:2]:
        copy.wait()
    place_v[...] = (near_places(dev_v[...], n_atmos, n_ocean) * tiles + tile_v[...]) * rows
    to_scalars = start_all(pltpu.make_async_copy(place_v, place, index_sems.at[0]))
    for copy in to_scalars + index[2:] + source:
        copy.wait()
    pairs = blocks.reshape(blocks.shape[0] // 2, 2 * blocks.shape[1], blocks.shape[2])
    for c in range(CHUNKS):
        weights[c].wait()
        block_sums(
            c * count, count, lambda b: b, lambda b, _: pairs[b // 2], lambda s: fields[s],
            lambda b: src[0, b], lambda b: place[0, b], total, rows,
        )
    for copy in late:
        copy.wait()
    surface[tiles * rows :, :] = mask[...].astype(F32)
    back_index[0] = near_places(back_v[0], n_atmos, n_ocean) * tiles + back_v[1]
    back_index[1] = back_v[2] * rows
    row = lax.axis_index("atm")
    same_side[...] = jnp.full_like(same_side, jnp.where(row % 2 == row // 2 % 2, 1, 0))


def run_step(count):
    return next(step for step in (24, 16, 8, 4) if count % step == 0)


def run_blocks(first, last, near, blocks, index, order, total, skipped):
    rows = near.shape[1]
    step = run_step(blocks.shape[0])

    def trip(at, carry):
        block_sums(
            at * step, step, lambda b: order[b],
            lambda b, c: jnp.concatenate([blocks[b], blocks[c]], axis=0), lambda s: near[s],
            lambda b: index[0, 0, b] - skipped, lambda b: index[1, 0, b], total, rows,
        )
        return carry

    lax.fori_loop(first, last, trip, 0)


def run_pairs(first, last, near, blocks, index, order, total):
    rows = near.shape[1]
    step = run_step(blocks.shape[0])
    odd = (last - first) % 2

    def trip(at, carry):
        block_sums(
            (first + odd + 2 * at) * step, 2 * step, lambda b: order[b],
            lambda b, c: jnp.concatenate([blocks[b], blocks[c]], axis=0), lambda s: near[s],
            lambda b: index[0, 0, b], lambda b: index[1, 0, b], total, rows,
        )
        return carry

    run_blocks(first, first + odd, near, blocks, index, order, total, 0)
    lax.fori_loop(0, (last - first) // 2, trip, 0)


def early_kernel(tiles, near, blocks, index_in, total, order_out, index, order, sems):
    count = blocks.shape[0]
    outer = 3 * tiles
    copy = pltpu.make_async_copy(index_in, index, sems.at[0])
    copy.start()
    total[...] = jnp.zeros_like(total)
    copy.wait()

    def place_block(b, ends):
        front, back = ends
        far = (index[0, 0, b] < outer).astype(jnp.int32)
        order[jnp.where(far == 1, back, front)] = b
        return front + 1 - far, back - far

    ready, _ = lax.fori_loop(0, count, place_block, (jnp.int32(0), jnp.int32(count - 1)), unroll=8)
    trips = ready // run_step(count)
    order[count] = trips
    copy = pltpu.make_async_copy(order, order_out, sems.at[0])
    copy.start()
    run_blocks(0, trips, near, blocks, index, order, total, outer)
    copy.wait()


def late_kernel(near, blocks, index_in, order_in, total_in, total, out, index, order, sems):
    count = blocks.shape[0]
    copies = start_all(
        pltpu.make_async_copy(index_in, index, sems.at[0]), pltpu.make_async_copy(order_in, order, sems.at[1])
    )
    for copy in copies:
        copy.wait()
    run_pairs(order[count], count // run_step(count), near, blocks, index, order, total)
    result = pltpu.make_async_copy(total, out, sems.at[0])
    result.start()
    result.wait()


def in_hbm(*arrays):
    return [pltpu.with_memory_space_constraint(a, pltpu.HBM) for a in arrays]


def hbm():
    return pl.BlockSpec(memory_space=pl.ANY)


def vmem():
    return pl.BlockSpec(memory_space=pltpu.VMEM)


def forward(n_atmos, n_ocean, atm_fields, fwd_blocks, index, state, mask, back_index):
    fields, cells = atm_fields.shape[1:]
    count = fwd_blocks.shape[0]
    tiles = state.shape[0]
    numbers = pltpu.VMEM((1, count), jnp.int32)
    scalars = pltpu.SMEM((1, count), jnp.int32)
    return pl.pallas_call(
        functools.partial(fwd_kernel, n_atmos, n_ocean),
        out_shape=[
            jax.ShapeDtypeStruct((9 * tiles * fields, cells), F32),
            jax.ShapeDtypeStruct((tiles * fields + tiles, cells), F32),
            jax.ShapeDtypeStruct((2, 1, count), jnp.int32),
            jax.ShapeDtypeStruct((1, 1, cells), jnp.int32),
        ],
        in_specs=[hbm()] * 10,
        out_specs=[vmem()] * 4,
        scratch_shapes=[
            pltpu.VMEM(fwd_blocks.shape, fwd_blocks.dtype),
            pltpu.VMEM(atm_fields.shape, atm_fields.dtype),
            pltpu.VMEM(mask.shape, mask.dtype),
            numbers, numbers, numbers,
            pltpu.VMEM((3, 1, count), jnp.int32),
            scalars, scalars,
            pltpu.SemaphoreType.DMA((CHUNKS,)),
            pltpu.SemaphoreType.DMA((9,)),
        ],
        compiler_params=pltpu.CompilerParams(vmem_limit_bytes=10 * 2**20),
        name="forward_blocks",
    )(*in_hbm(atm_fields, fwd_blocks, *index, state.reshape(tiles * fields, cells), mask, *back_index))


def backward_early(near, back_blocks, index, tiles, atmos_count):
    fields, cells = near.shape[1:]
    count = back_blocks.shape[0]
    listed = (count + 64,)
    return pl.pallas_call(
        functools.partial(early_kernel, tiles),
        out_shape=[
            jax.ShapeDtypeStruct((atmos_count * fields, cells), F32),
            jax.ShapeDtypeStruct(listed, jnp.int32),
        ],
        in_specs=[vmem()] * 3,
        out_specs=[vmem(), vmem()],
        scratch_shapes=[
            pltpu.SMEM(index.shape, jnp.int32),
            pltpu.SMEM(listed, jnp.int32),
            pltpu.SemaphoreType.DMA((1,)),
        ],
        compiler_params=pltpu.CompilerParams(vmem_limit_bytes=4 * 2**20),
        name="early_blocks",
    )(near, back_blocks, index)


def backward_late(near, back_blocks, index, order, total):
    fields, cells = near.shape[1:]
    shape = jax.ShapeDtypeStruct(total.shape, F32)
    _, out = pl.pallas_call(
        late_kernel,
        out_shape=[shape, shape],
        in_specs=[vmem()] * 5,
        out_specs=[vmem(), hbm()],
        scratch_shapes=[
            pltpu.SMEM(index.shape, jnp.int32),
            pltpu.SMEM(order.shape, jnp.int32),
            pltpu.SemaphoreType.DMA((2,)),
        ],
        input_output_aliases={4: 0},
        compiler_params=pltpu.CompilerParams(vmem_limit_bytes=4 * 2**20),
        name="backward_blocks",
    )(near, back_blocks, index, order, total)
    return out.reshape(-1, fields, cells)


def ring_pairs(count, stride, inner):
    pairs = []
    for i in range(count):
        step = stride if (i // stride % 2 == 0) == inner else -stride
        pairs.append((i, (i + step) % count))
    return pairs


def swap(block, axis, stride, inner):
    return lax.ppermute(block, axis, ring_pairs(lax.axis_size(axis), stride, inner))


def shards(
    atm_fields, fwd_blocks, fwd_src_tile, fwd_dst_dev, fwd_dst_tile, ocean_state, wet_mask,
    back_blocks, back_src_dev, back_src_tile, back_dst_tile,
):
    n_atmos = lax.axis_size("atm")
    n_ocean = lax.axis_size("ocn")
    fields, cells = atm_fields.shape[1:]
    ocean_count = ocean_state.shape[0]
    atmos_count = atm_fields.shape[0]
    flat = (1, fwd_src_tile.shape[0])
    totals, surface, index, same_side = forward(
        n_atmos, n_ocean, atm_fields, fwd_blocks,
        [a.reshape(flat) for a in (fwd_src_tile, fwd_dst_dev, fwd_dst_tile)],
        ocean_state, wet_mask,
        [a.reshape(flat) for a in (back_src_dev, back_src_tile, back_dst_tile)],
    )
    outer_col, own, inner_col = totals.reshape(3, 3, ocean_count, fields, cells)
    from_inner = swap((inner_col * FIRST_SCALE).astype(F16), "ocn", 1, True)
    from_outer = swap((outer_col * FIRST_SCALE).astype(F16), "ocn", 1, False)
    row_sums = own + (from_inner.astype(F32) + from_outer.astype(F32)) * (1.0 / FIRST_SCALE)
    sent = (row_sums * SECOND_SCALE).astype(F16)
    same = same_side > 0
    to_inner = jnp.where(same, sent[2], sent[0])
    to_outer = jnp.where(same, sent[0], sent[2])
    inner_state = swap(surface, "atm", 1, True)
    outer_state = swap(surface, "atm", 1, False)
    inner = swap(sent[1:], "atm", 1, True)
    outer = swap(sent[:2], "atm", 1, False)
    far_inner = swap(to_inner, "atm", 2, True)
    far_outer = swap(to_outer, "atm", 2, False)
    direct = jnp.stack([outer[1], inner[1], inner[0]]).astype(F32)
    other = jnp.stack([jnp.where(same, far_outer, far_inner), outer[0], jnp.where(same, far_inner, far_outer)]).astype(F32)
    sums = row_sums + (direct + other) * (1.0 / SECOND_SCALE)
    surface = jnp.stack([outer_state, surface, inner_state])
    state = surface[:, : ocean_count * fields].reshape(sums.shape)
    wet = surface[:, ocean_count * fields :].reshape(3, ocean_count, 1, cells)
    response = (wet * jnp.tanh(state + sums)).astype(jnp.bfloat16)
    inner_near = swap(response, "ocn", 1, True)
    outer_near = swap(response, "ocn", 1, False)
    ready = jnp.stack([response, inner_near]).reshape(6 * ocean_count, fields, cells)
    total, order = backward_early(ready, back_blocks, index, ocean_count, atmos_count)
    near = jnp.stack([outer_near, response, inner_near]).reshape(9 * ocean_count, fields, cells)
    return (sums[1], backward_late(near, back_blocks, index, order, total))


def solution(mesh):
    part = ("atm", "ocn")
    three, two, one = P(part, None, None), P(part, None), P(part)
    in_specs = (three, three, one, two, one, three, two, three, two, one, one)
    return jax.shard_map(shards, mesh=mesh, in_specs=in_specs, out_specs=(three, three), check_vma=False)
```
